32 devices in a mesh: row: 4 (over y, x), col: 4 (over z), img: 2 (over core).
Axes of the slice: x: 2, y: 2, z: 4, core: 2. Of those that a mesh axis runs over, the one named last changes fastest.
Arguments:
- student: bfloat16 [2, 1024, 4096], P('img', 'col', 'row'), may hold values from -6 to 6
- teacher: bfloat16 [2, 1024, 4096], P('img', 'col', 'row'), may hold values from -6 to 6
Outputs:
- feature_grad: bfloat16 [2, 1024, 4096], P('img', 'col', 'row')
The draws below stay inside these ranges and needn't reach their ends.
All inputs are finite; a program needn't handle non-finite values.
Results may differ from the reference program's by a relative error of at most 0.012.
Values may be sent and summed in bfloat16 or wider, within the bound.
No kernel may reach another device: no remote copies, remote signals or barrier semaphores. Data moves between devices by JAX's collectives and lax.ppermute only.
A program may use at most 64 MiB of HBM per device.

```python
import jax
import jax.numpy as jnp
from jax import lax

D = 4096
PB = 256
PATCHES = 1024
IMAGES = 2
N_COL = 4


def levels(key, dims, shards, low, largest):
    def one(axis_at, shards_of):
        heights = jax.random.uniform(jax.random.fold_in(jax.random.fold_in(key, 6), axis_at), (shards_of,), jnp.float32, low / len(shards), largest / len(shards))
        return jnp.repeat(jnp.exp(heights), dims[axis_at] // shards_of).reshape((-1,) + (1,) * (len(dims) - axis_at - 1))

    factor_of = one(*shards[0])
    for cut in shards[1:]:
        factor_of = factor_of * one(*cut)
    return factor_of


def scatter_about(stream_key, dims, scale, most, shards=(), held_as=jnp.bfloat16):
    values = scale * jax.random.normal(stream_key, dims, jnp.float32)
    if shards:
        values = values * levels(stream_key, dims, shards, -0.22, 0.18)
    return jnp.clip(values, -most, most).astype(held_as)


def setup_inputs(seed: int = 0) -> dict:
    key_of = jax.random.split(jax.random.key(seed), 3)
    return {
        "student": scatter_about(key_of[0], (IMAGES, PATCHES, D), 1.0, 6.0, ((0, 2), (1, 4), (2, 4))),
        "teacher": scatter_about(key_of[1], (IMAGES, PATCHES, D), 1.0, 6.0, ((0, 2), (1, 4), (2, 4))),
    }


def one_image(pair):
    xs, xt = pair
    xs32 = xs.astype(jnp.float32)
    xt32 = xt.astype(jnp.float32)
    gram_student = jnp.dot(xs32, xs32.T) / D
    gram_teacher = jnp.dot(xt32, xt32.T) / D
    gap = (gram_student - gram_teacher).astype(jnp.bfloat16).astype(jnp.float32)
    gap_rows = gap.reshape(N_COL, PB, PB * N_COL)
    feat_rows = xs32.reshape(N_COL, PB, D)

    def accumulate(total, blocks):
        gap_block, feat_block = blocks
        part = jnp.dot(gap_block.T, feat_block).astype(jnp.bfloat16)
        return total + part.astype(jnp.float32), None

    total, unused = lax.scan(accumulate, jnp.zeros((PB * N_COL, D), jnp.float32), (gap_rows, feat_rows))
    return total.astype(jnp.bfloat16)


def reference(student, teacher):
    return lax.map(one_image, (student, teacher))
```

```python
import functools

import jax
import jax.numpy as jnp
from jax import lax
from jax.experimental import pallas as pl
from jax.experimental.pallas import tpu as pltpu
from jax.sharding import PartitionSpec as P

AXES = ("row", "col", "img")
NT = (((1,), (1,)), ((), ()))
NN = (((1,), (0,)), ((), ()))
TN = (((0,), (0,)), ((), ()))
VMEM = pltpu.MemorySpace.VMEM


def dot(a, b, dims):
    return lax.dot_general(a, b, dims, preferred_element_type=jnp.float32)


def place(n_col):
    col = lax.axis_index("col")
    return jnp.where(lax.axis_index("img") % 2 == 1, n_col - 1 - col, col)


def gram_kernel(pairs, n_row, names, *refs):
    count = len(names)
    s = dict(zip(names, refs[:count]))
    t = dict(zip(names, refs[count : 2 * count]))
    outs, block = refs[2 * count : -1], refs[-1]
    me = lax.axis_index("row")
    rows = block.shape[0] // n_row
    for at, (i, j) in enumerate(pairs):
        block[...] = dot(s[i][...], s[j][...], NT) - dot(t[i][...], t[j][...], NT)
        for k, out in enumerate(outs):
            start = pl.multiple_of((me ^ k) * rows, rows)
            out[at] = block[pl.ds(start, rows), :].astype(out.dtype)


def gram(pairs, n_row, s, t):
    names = tuple(sorted(s))
    size, depth = s[names[0]].shape
    shape = jax.ShapeDtypeStruct((len(pairs), size // n_row, size), jnp.bfloat16)
    flops = 4 * len(pairs) * size * size * depth
    moved = 2 * (2 * len(names) * size * depth + len(pairs) * size * size)
    return pl.pallas_call(
        functools.partial(gram_kernel, pairs, n_row, names),
        out_shape=[shape] * n_row,
        in_specs=[pl.BlockSpec(memory_space=VMEM)] * (2 * len(names)),
        out_specs=[pl.BlockSpec(memory_space=VMEM)] * n_row,
        scratch_shapes=[pltpu.VMEM((size, size), jnp.float32)],
        cost_estimate=pl.CostEstimate(flops=flops, bytes_accessed=moved, transcendentals=0),
    )(*[s[i] for i in names], *[t[i] for i in names])


def sum_kernel(n_col, n_row, width, chunks, *refs):
    outs = refs[-n_col:]
    at = 0
    for pairs in chunks:
        group = refs[at : at + n_row]
        at += n_row
        for b, (i, j) in enumerate(pairs):
            total = group[0][b].astype(jnp.float32)
            for other in group[1:]:
                total += other[b].astype(jnp.float32)
            total = (total / width).astype(jnp.bfloat16)
            outs[i][j] = total
            if i != j:
                outs[j][i] = total


def add_up(n_col, n_row, width, chunks, parts):
    rows, size = parts[0].shape[1:]
    shape = jax.ShapeDtypeStruct((n_col, rows, size), jnp.bfloat16)
    count = sum(len(pairs) for pairs in chunks)
    return pl.pallas_call(
        functools.partial(sum_kernel, n_col, n_row, width, chunks),
        out_shape=[shape] * n_col,
        in_specs=[pl.BlockSpec(memory_space=VMEM)] * len(parts),
        out_specs=[pl.BlockSpec(memory_space=VMEM)] * n_col,
        cost_estimate=pl.CostEstimate(
            flops=n_row * count * rows * size,
            bytes_accessed=2 * (n_row * count + n_col * n_col) * rows * size,
            transcendentals=0,
        ),
    )(*parts)


def final_kernel(n_col, n_row, *refs):
    gaps, own, rest = refs[:n_row], refs[n_row], refs[n_row + 1 : -3]
    lefts, rights = rest[: n_col - 1], rest[n_col - 1 :]
    out, block, total = refs[-3:]
    me, z = lax.axis_index("row"), place(n_col)
    rows = gaps[0].shape[1]

    def load(at):
        for k, gap in enumerate(gaps):
            start = pl.multiple_of((me ^ k) * rows, rows)
            block[pl.ds(start, rows), :] = gap[at]

    load(z)
    total[...] = dot(block[...], own[...], NN)
    for k in range(1, n_col):

        @pl.when(z + k < n_col)
        def _():
            load(z + k)
            total[...] += dot(block[...], lefts[k - 1][...], TN)

        @pl.when(z - k >= 0)
        def _():
            load(z - k)
            total[...] += dot(block[...], rights[k - 1][...], NN)

    out[...] = total[...].astype(out.dtype)


def finish(n_col, n_row, gaps, own, lefts, rights):
    size, depth = own.shape
    args = (*gaps, own, *lefts, *rights)
    return pl.pallas_call(
        functools.partial(final_kernel, n_col, n_row),
        out_shape=jax.ShapeDtypeStruct((size, depth), jnp.bfloat16),
        in_specs=[pl.BlockSpec(memory_space=VMEM)] * len(args),
        out_specs=pl.BlockSpec(memory_space=VMEM),
        scratch_shapes=[pltpu.VMEM((size, size), jnp.bfloat16), pltpu.VMEM((size, depth), jnp.float32)],
        cost_estimate=pl.CostEstimate(
            flops=2 * n_col * size * size * depth,
            bytes_accessed=2 * (2 * n_col * size * depth + n_col * size * size),
            transcendentals=0,
        ),
    )(*args)


def body(student, teacher):
    n_row, n_col, n_img = (lax.axis_size(a) for a in AXES)
    width = student.shape[2] * n_row
    own_s = student.reshape(student.shape[1:])
    own_t = teacher.reshape(teacher.shape[1:])
    hub, last = n_col // 2 - 1, n_col - 1
    z = place(n_col)

    def index(row, at, img):
        col = n_col - 1 - at if img % 2 else at
        return (row * n_col + col) * n_img + img

    def along_col(x, pairs):
        perm = [
            (index(r, a, g), index(r, b, g)) for r in range(n_row) for g in range(n_img) for a, b in pairs
        ]
        return lax.ppermute(x, AXES, perm)

    def along_row(x, k, places):
        perm = [
            (index(r, a, g), index(r ^ k, a, g)) for r in range(n_row) for g in range(n_img) for a in places
        ]
        return lax.ppermute(x, AXES, perm)

    t, s = {hub: own_t}, {hub: own_s}
    for p in range(last, hub, -1):
        t[p] = along_col(own_t, [(p, hub)])
    lefts = [along_col(own_s, [(i + 1, i) for i in range(last)])]
    held_s, held_t, _ = lax.optimization_barrier((own_s, own_t, lefts[0]))
    for p in range(hub):
        t[p] = along_col(held_t, [(p, hub)])
    early, x = [], held_s
    for k in range(1, hub + 1):
        x = along_col(x, [(i, i + 1) for i in range(k - 1, hub)])
        early.append(x)
        s[hub - k] = x
    s[hub + 1] = lefts[0]
    for k in range(2, n_col - hub):
        lefts.append(along_col(lefts[-1], [(i + 1, i) for i in range(n_col - k)]))
        s[hub + k] = lefts[-1]

    pairs_a = tuple((i, j) for i in range(last) for j in range(i + 1))
    pairs_b = tuple((last, j) for j in range(n_col))
    parts = []
    for pairs in (pairs_a, pairs_b):
        used = {p for pair in pairs for p in pair}
        sent = gram(pairs, n_row, {p: s[p] for p in used}, {p: t[p] for p in used})
        parts.append(sent[0])
        parts.extend(along_row(sent[k], k, (hub,)) for k in range(1, n_row))

    late_s, *_ = lax.optimization_barrier((own_s, lefts[-1], t[0]))
    for k in range(n_col - hub, n_col):
        lefts.append(along_col(lefts[-1], [(i + 1, i) for i in range(n_col - k)]))
    rights, x = [], late_s
    for k in range(1, n_col):
        x = along_col(x, [(i, i + 1) for i in range(max(hub, k - 1), last)])
        if k <= hub:
            x = x + early[k - 1]
        rights.append(x)

    quarters = add_up(n_col, n_row, width, (pairs_a, pairs_b), parts)
    mine = jnp.where(z == hub, quarters[hub], jnp.zeros_like(quarters[hub]))
    for p in range(n_col):
        if p != hub:
            mine = mine + along_col(quarters[p], [(hub, p)])
    gaps = [mine] + [along_row(mine, k, range(n_col)) for k in range(1, n_row)]
    out = finish(n_col, n_row, gaps, own_s, lefts, rights)
    return out.reshape(student.shape)


def solution(mesh):
    placed = (P("img", "col", "row"), P("img", "col", "row"))
    return jax.shard_map(
        body, mesh=mesh, in_specs=placed, out_specs=P("img", "col", "row"), check_vma=False
    )
```
